32 devices in a mesh: fsdp: 2 (over core), ctx: 8 (over z, y), tp: 2 (over x).
Axes of the slice: x: 2, y: 2, z: 4, core: 2. Of those that a mesh axis runs over, the one named last changes fastest.
Arguments:
- tokens: bfloat16 [2, 2048, 512], P('fsdp', 'ctx'), may hold values from -11 to 11
- source_states: bfloat16 [2, 1024, 512], P('fsdp', 'ctx'), may hold values from -6 to 6
- block_ids: int32 [2, 2048], P('fsdp', 'ctx'), may hold values from 0 to 15, never falling along the last dimension, each value on 1 to 256 neighbouring positions
- source_len: int32 [2], P('fsdp'), may hold values from 256 to 1024, as said below
- out_grad: bfloat16 [2, 2048, 512], P('fsdp', 'ctx'), may hold values from -6 to 6
- self_qkv: bfloat16 [3, 512, 512], P(None, 'fsdp', 'tp'), may hold values from -0.25 to 0.25
- self_out: bfloat16 [512, 512], P('tp', 'fsdp'), may hold values from -0.75 to 0.75
- cross_q: bfloat16 [512, 512], P('fsdp', 'tp'), may hold values from -0.25 to 0.25
- cross_kv: bfloat16 [2, 512, 512], P(None, 'fsdp', 'tp'), may hold values from -0.25 to 0.25
- cross_out: bfloat16 [512, 512], P('tp', 'fsdp'), may hold values from -1 to 1
- ffn_in: bfloat16 [512, 2048], P('fsdp', 'tp'), may hold values from -0.25 to 0.25
- ffn_out: bfloat16 [2048, 512], P('tp', 'fsdp'), may hold values from -0.125 to 0.125
- attn_bias: float32 [4, 512], P('fsdp', 'tp'), may hold values from -3 to 3
- ffn_in_bias: float32 [2048], P('tp'), may hold values from -3 to 3
- out_bias: float32 [3, 512], P(None, 'fsdp'), may hold values from -2 to 2
- norm_gain: float32 [3, 512], P(None, 'fsdp'), may hold values from 0.5 to 1.5
- norm_bias: float32 [3, 512], P(None, 'fsdp'), may hold values from -2 to 2
Outputs:
- output: bfloat16 [2, 2048, 512], P('fsdp', 'ctx')
- input_grad: float32 [2, 2048, 512], P('fsdp', 'ctx')
- source_grad: float32 [2, 1024, 512], P('fsdp', 'ctx')
- rms_values: float32 [4], replicated
- grad_self_qkv: float32 [3, 512, 512], P(None, 'fsdp', 'tp')
- grad_self_out: float32 [512, 512], P('tp', 'fsdp')
- grad_cross_q: float32 [512, 512], P('fsdp', 'tp')
- grad_cross_kv: float32 [2, 512, 512], P(None, 'fsdp', 'tp')
- grad_cross_out: float32 [512, 512], P('tp', 'fsdp')
- grad_ffn_in: float32 [512, 2048], P('fsdp', 'tp')
- grad_ffn_out: float32 [2048, 512], P('tp', 'fsdp')
- grad_attn_bias: float32 [4, 512], P('fsdp', 'tp')
- grad_ffn_in_bias: float32 [2048], P('tp')
- grad_out_bias: float32 [3, 512], P(None, 'fsdp')
- grad_norm_gain: float32 [3, 512], P(None, 'fsdp')
- grad_norm_bias: float32 [3, 512], P(None, 'fsdp')
The draws below stay inside these ranges and needn't reach their ends.
Inputs may be any that keep to these rules, and one draw needn't show every extreme that they name: `block_ids`: along each sequence the ids never fall; each id covers 1 to 256 consecutive positions, and one covers exactly 256. `source_len`: some sequence uses all 1024 source positions.
All inputs are finite; a program needn't handle non-finite values.
Results may differ from the reference program's by a relative error of at most 0.03.
Values may be sent and summed in bfloat16 or wider, within the bound.
No kernel may reach another device: no remote copies, remote signals or barrier semaphores. Data moves between devices by JAX's collectives and lax.ppermute only.
A program may use at most 128 MiB of HBM per device.

```python
import math
import jax
import jax.numpy as jnp
import numpy as np
from jax import lax

D = 512
HEADS = 8
HEAD = 64
FF = 2048
SRC = 1024
BLOCK = 256
SEQS = 2
LENGTH = 2048


def draw_source_len(key, part):
    first_key, second_key = jax.random.split(jax.random.fold_in(key, 7))
    lengths = jax.random.randint(first_key, (SEQS,), SRC // 4, SRC + 1)
    longest = jax.random.randint(second_key, (), 0, SEQS)
    return jnp.where(jnp.arange(SEQS) == longest, SRC, lengths).astype(jnp.int32)


def draw_tokens(key, part):
    inner = jax.random.fold_in(key, 11)
    place = (jnp.arange(SEQS, dtype=jnp.float32)[:, None] * LENGTH + jnp.arange(LENGTH, dtype=jnp.float32)[None, :]) / (SEQS * LENGTH)
    noise = jnp.clip(jax.random.normal(inner, (SEQS, LENGTH, D), jnp.float32), -6.0, 6.0)
    scale = 0.6 * jnp.exp(1.0986123 * place)
    return (noise * scale[:, :, None]).astype(jnp.bfloat16)


def block_levels(own_key, shape, cuts, smallest, high):
    level = 1.0
    for axis_at, blocks in cuts:
        draws = jax.random.uniform(jax.random.fold_in(jax.random.fold_in(own_key, 6), axis_at), (blocks,), jnp.float32, smallest / len(cuts), high / len(cuts))
        level = level * jnp.repeat(jnp.exp(draws), shape[axis_at] // blocks).reshape((-1,) + (1,) * (len(shape) - 1 - axis_at))
    return level


def profile(number_of, total, most, slope):
    portions = [(1 << 20) // math.isqrt(rank ** slope) + 1 for rank in range(2, number_of + 1)]
    spare, given = total - most - (number_of - 1), [1] * (number_of - 1)
    while spare > 0:
        movable = [i for i in range(number_of - 1) if given[i] < most]
        mass, remaining = sum([portions[i] for i in movable]), spare
        for i in movable:
            extra = min(most - given[i], max(1, remaining * portions[i] // mass), spare)
            given[i] = given[i] + extra
            spare = spare - extra
    return np.array([most] + given)


def ragged_sizes(rng, amount, total, bound, skew):
    if amount == 2:
        one = jax.random.randint(rng, (), max(1, total - bound), min(bound, total - 1) + 1)
        return jnp.stack([one, total - one])
    tallies = jnp.asarray(profile(amount, total, bound, skew), jnp.int32)
    pairs = (amount - 1) // 2
    donor, taker = tallies[1:1 + 2 * pairs:2], tallies[2:2 + 2 * pairs:2]
    margin = jnp.minimum(donor - 1, bound - taker)
    passed = jax.random.randint(jax.random.fold_in(rng, 1), (pairs,), 0, 1 << 20) % (margin + 1)
    tallies = tallies.at[1:1 + 2 * pairs:2].set(donor - passed).at[2:2 + 2 * pairs:2].set(taker + passed)
    return tallies[jax.random.permutation(jax.random.fold_in(rng, 2), amount)]


def scatter_about(key, dims, deviation, bound, shards=(), held_as=jnp.bfloat16):
    drawn = jax.random.normal(key, dims, jnp.float32) * deviation
    if len(shards) > 0:
        drawn = block_levels(key, dims, shards, -0.22, 0.18) * drawn
    return jnp.clip(drawn, min=-bound, max=bound).astype(held_as)


def setup_inputs(seed: int = 0) -> dict:
    key_list = jax.random.split(jax.random.key(seed), 18)
    return {
        "tokens": draw_tokens(jax.random.fold_in(key_list[17], 71), 0),
        "source_states": scatter_about(key_list[1], (SEQS, SRC, D), 1.0, 6.0, ((0, 2), (1, 8))),
        "block_ids": jax.vmap(lambda own: jnp.searchsorted(jnp.cumsum(ragged_sizes(own, 2 * LENGTH // BLOCK, LENGTH, BLOCK, 0)), jnp.arange(LENGTH), side="right"))(jax.random.split(key_list[2], SEQS)).reshape((SEQS, LENGTH)).astype(jnp.int32),
        "source_len": draw_source_len(jax.random.fold_in(key_list[17], 71), 0),
        "out_grad": scatter_about(key_list[4], (SEQS, LENGTH, D), 1.0, 6.0, ((0, 2), (1, 8))),
        "self_qkv": scatter_about(key_list[5], (3, D, D), D ** -0.5, 0.25, ((1, 2), (2, 2))),
        "self_out": scatter_about(key_list[6], (D, D), (max(1, D * 256 // LENGTH)) ** -0.5, 0.75, ((0, 2), (1, 2))),
        "cross_q": scatter_about(key_list[7], (D, D), D ** -0.5, 0.25, ((0, 2), (1, 2))),
        "cross_kv": scatter_about(key_list[8], (2, D, D), D ** -0.5, 0.25, ((1, 2), (2, 2))),
        "cross_out": scatter_about(key_list[9], (D, D), (D // 16) ** -0.5, 1.0, ((0, 2), (1, 2))),
        "ffn_in": scatter_about(key_list[10], (D, FF), D ** -0.5, 0.25, ((0, 2), (1, 2))),
        "ffn_out": scatter_about(key_list[11], (FF, D), FF ** -0.5, 0.125, ((0, 2), (1, 2))),
        "attn_bias": scatter_about(key_list[12], (4, D), 0.5, 3.0, ((0, 2), (1, 2)), jnp.float32),
        "ffn_in_bias": scatter_about(key_list[13], (FF,), 0.5, 3.0, ((0, 2),), jnp.float32),
        "out_bias": scatter_about(key_list[14], (3, D), 0.3, 2.0, ((1, 2),), jnp.float32),
        "norm_gain": jnp.clip(1.0 + 0.1 * jax.random.normal(key_list[15], (3, D), jnp.float32), 0.5, 1.5),
        "norm_bias": scatter_about(key_list[16], (3, D), 0.3, 2.0, ((1, 2),), jnp.float32),
    }


@jax.custom_vjp
def low(v):
    return lax.optimization_barrier(v.astype(jnp.bfloat16)).astype(jnp.float32)

@jax.custom_vjp
def low_back(v):
    return v

def low_keep(v):
    return (low(v), None)

def low_pass(kept, grad):
    return (grad,)

def back_keep(v):
    return (v, None)

def back_low(kept, grad):
    return (low(grad),)
low.defvjp(low_keep, low_pass)
low_back.defvjp(back_keep, back_low)
HIGH = lax.Precision.HIGHEST
NEG = -1e+30
EPSILON = 1e-05

def matmul(left, right):
    return jnp.dot(left, right, precision=HIGH, preferred_element_type=jnp.float32)

def rounded(value):
    return low_back(low(value))

def layer_norm(resid, gain, shift):
    average = lax.optimization_barrier(jnp.mean(resid, axis=-1, keepdims=True))
    centred = resid - average
    variance = lax.optimization_barrier(jnp.mean(centred * centred, axis=-1, keepdims=True))
    return centred * lax.rsqrt(variance + EPSILON) * gain + shift

def softmax_rows(scores):
    top = lax.optimization_barrier(jnp.max(scores, axis=-1, keepdims=True))
    powers = jnp.exp(scores - top)
    return powers / lax.optimization_barrier(jnp.sum(powers, axis=-1, keepdims=True))

def attend(queries, keys, values, allowed):
    scores = jnp.einsum('qhd,khd->qhk', queries, keys, precision=HIGH) * HEAD ** (-0.5)
    scores = low_back(scores)
    weights = softmax_rows(jnp.where(allowed, scores, NEG))
    return jnp.einsum('qhk,khd->qhd', low(weights), values, precision=HIGH)

def self_attention(queries, keys, values, segment):
    rows = queries.shape[0]
    width = 512 if rows % 512 == 0 else rows
    count = rows // width
    query_heads = queries.reshape(count, width, HEADS, HEAD)
    query_segs = segment.reshape(count, width)
    key_heads = keys.reshape(rows, HEADS, HEAD)
    value_heads = values.reshape(rows, HEADS, HEAD)

    def one_block(block):
        block_q, block_seg = block
        allowed = segment[None, None, :] <= block_seg[:, None, None]
        return attend(block_q, key_heads, value_heads, allowed)
    result = lax.map(jax.checkpoint(one_block), (query_heads, query_segs))
    return result.reshape(rows, D)

def one_sequence(inputs, states, segment, length, params):
    self_qkv, self_out, cross_q, cross_kv, cross_out, ffn_in, ffn_out, attn_bias, ffn_in_bias, out_bias, norm_gain, norm_bias = params
    queries = rounded(matmul(inputs, self_qkv[0]) + attn_bias[0])
    keys = rounded(matmul(inputs, self_qkv[1]))
    values = rounded(matmul(inputs, self_qkv[2]) + attn_bias[1])
    mixed = rounded(self_attention(queries, keys, values, segment))
    self_branch = low_back(matmul(mixed, self_out)) + out_bias[0]
    first = layer_norm(inputs + self_branch, norm_gain[0], norm_bias[0])
    cross_query = rounded(matmul(low(first), cross_q) + attn_bias[2])
    cross_keys = rounded(matmul(states, cross_kv[0]))
    cross_values = rounded(matmul(states, cross_kv[1]) + attn_bias[3])
    allowed = (jnp.arange(SRC) < length)[None, None, :]
    looked = attend(cross_query.reshape(-1, HEADS, HEAD), cross_keys.reshape(SRC, HEADS, HEAD), cross_values.reshape(SRC, HEADS, HEAD), allowed)
    looked = rounded(looked.reshape(-1, D))
    cross_branch = low_back(matmul(looked, cross_out)) + out_bias[1]
    second = layer_norm(first + cross_branch, norm_gain[1], norm_bias[1])
    hidden = low_back(matmul(low(second), ffn_in) + ffn_in_bias)
    active = low(hidden / (1.0 + jnp.exp(-hidden)))
    ffn_branch = low_back(matmul(active, ffn_out)) + out_bias[2]
    result = layer_norm(second + ffn_branch, norm_gain[2], norm_bias[2])
    squares = jnp.stack([jnp.sum(inputs * inputs), jnp.sum(self_branch * self_branch), jnp.sum(cross_branch * cross_branch), jnp.sum(ffn_branch * ffn_branch)])
    return (result, squares)

def reference(tokens, source_states, block_ids, source_len, out_grad, self_qkv, self_out, cross_q, cross_kv, cross_out, ffn_in, ffn_out, attn_bias, ffn_in_bias, out_bias, norm_gain, norm_bias):
    params = tuple((item.astype(jnp.float32) for item in (self_qkv, self_out, cross_q, cross_kv, cross_out, ffn_in, ffn_out, attn_bias, ffn_in_bias, out_bias, norm_gain, norm_bias)))

    def forward(inputs, states, *weights):
        results = []
        totals = jnp.zeros((4,), jnp.float32)
        for index in range(SEQS):
            result, squares = one_sequence(inputs[index], states[index], block_ids[index], source_len[index], weights)
            results.append(result)
            totals = totals + squares
        return (jnp.stack(results), totals)
    output, pullback, totals = jax.vjp(forward, tokens.astype(jnp.float32), source_states.astype(jnp.float32), *params, has_aux=True)
    grads = pullback(out_grad.astype(jnp.float32))
    rms_values = jnp.sqrt(totals / (SEQS * LENGTH * D))
    return (output.astype(jnp.bfloat16), grads[0], grads[1], rms_values, grads[2], grads[3], grads[4], grads[5], grads[6], grads[7], grads[8], grads[9], grads[10], grads[11], grads[12], grads[13])
```

```python
import jax
import jax.numpy as jnp
from jax import lax
from jax.sharding import PartitionSpec as P

HEAD = 64


NEG = -1e30
EPSILON = 1e-05


def cut_along(x, dim, devices):
    before, after = (x.shape[:dim], x.shape[dim + 1 :])
    return jnp.moveaxis(x.reshape(*before, devices, -1, *after), dim, 0)


def sum_at_owner(x, axis, dim):
    pieces = cut_along(x, dim, lax.axis_size(axis))
    arrived = lax.all_to_all(pieces, axis, split_axis=0, concat_axis=0, tiled=True)
    return arrived.astype(jnp.float32).sum(axis=0)


def in_one_piece(arrays, axis, dim, along):
    both = jnp.concatenate(arrays, axis=along)
    out, at, done = (sum_at_owner(both, axis, dim), 0, [])
    for a in arrays:
        done.append(lax.slice_in_dim(out, at, at + a.shape[along], axis=along))
        at += a.shape[along]
    return tuple(done)


def other(axis):
    size = lax.axis_size(axis)
    return [(i, (i + size // 2) % size) for i in range(size)]


def tp_total(part):
    return part.astype(jnp.float32) + lax.ppermute(part, "tp", other("tp")).astype(jnp.float32)


def pair_scatter(x, dim):
    half = x.shape[dim] // 2
    me = lax.axis_index("fsdp")
    sent = lax.dynamic_slice_in_dim(x, (1 - me) * half, half, dim).astype(jnp.bfloat16)
    kept = lax.dynamic_slice_in_dim(x, me * half, half, dim)
    return kept + lax.ppermute(sent, "fsdp", other("fsdp")).astype(jnp.float32)


def gather_by_exchange(x, axis):
    size = lax.axis_size(axis)
    return lax.all_to_all(
        jnp.broadcast_to(x[None], (size,) + x.shape), axis, split_axis=0, concat_axis=0, tiled=True
    )


def ctx_total(x):
    size = lax.axis_size("ctx")
    pieces = x.reshape(size, -1, x.shape[1])
    arrived = lax.all_to_all(pieces, "ctx", split_axis=0, concat_axis=0, tiled=True)
    mine = arrived.astype(jnp.float32).sum(axis=0).astype(jnp.bfloat16)
    return gather_by_exchange(mine, "ctx").reshape(x.shape)


def matmul(left, right):
    return jnp.dot(left, right, preferred_element_type=jnp.float32)


def matmul_tn(left, right):
    return lax.dot_general(
        left, right, (((0,), (0,)), ((), ())), preferred_element_type=jnp.float32
    )


def matmul_nt(left, right):
    return lax.dot_general(
        left, right, (((1,), (1,)), ((), ())), preferred_element_type=jnp.float32
    )


def split_heads(matrix):
    return matrix.reshape(matrix.shape[0], matrix.shape[1] // HEAD, HEAD)


def norm_forward(resid, gain, shift):
    average = jnp.mean(resid, axis=-1, keepdims=True)
    centred = resid - average
    inverse = lax.rsqrt(jnp.mean(centred * centred, axis=-1, keepdims=True) + EPSILON)
    normed = centred * inverse
    return (normed * gain + shift, normed, inverse)


def norm_backward(grad_out, normed, inverse, gain):
    grad_norm = grad_out * gain
    first_mean = jnp.mean(grad_norm, axis=-1, keepdims=True)
    second_mean = jnp.mean(grad_norm * normed, axis=-1, keepdims=True)
    grad_in = inverse * (grad_norm - first_mean - normed * second_mean)
    return (grad_in, jnp.sum(grad_out * normed, axis=0), jnp.sum(grad_out, axis=0))


def in_blocks(items):
    count = items[0].shape[0]
    width = 512
    return tuple((item.reshape((count // width, width) + item.shape[1:]) for item in items))


def pass_state(state):
    return state


def scores_of(query_heads, key_heads, query_segs, key_segs):
    scores = jnp.einsum(
        "qhd,khd->qhk", query_heads, key_heads, preferred_element_type=jnp.float32
    ) * HEAD ** (-0.5)
    allowed = key_segs[None, None, :] <= query_segs[:, None, None]
    return jnp.where(allowed, scores, NEG)


def per_device(
    tokens,
    source_states,
    block_ids,
    source_len,
    out_grad,
    self_qkv,
    self_out,
    cross_q,
    cross_kv,
    cross_out,
    ffn_in,
    ffn_out,
    attn_bias,
    ffn_in_bias,
    out_bias,
    norm_gain,
    norm_bias,
):
    w_qkv, w_out, w_cq, w_ckv, w_co, w_in, w_fout, b_attn, b_out, gains, shifts = (
        lax.all_gather(self_qkv, "fsdp", axis=1, tiled=True),
        lax.all_gather(self_out, "fsdp", axis=1, tiled=True),
        lax.all_gather(cross_q, "fsdp", axis=0, tiled=True),
        lax.all_gather(cross_kv, "fsdp", axis=1, tiled=True),
        lax.all_gather(cross_out, "fsdp", axis=1, tiled=True),
        lax.all_gather(ffn_in, "fsdp", axis=0, tiled=True),
        lax.all_gather(ffn_out, "fsdp", axis=1, tiled=True),
        lax.all_gather(attn_bias.astype(jnp.bfloat16), "fsdp", axis=0, tiled=True).astype(
            attn_bias.dtype
        ),
        lax.all_gather(out_bias.astype(jnp.bfloat16), "fsdp", axis=1, tiled=True).astype(
            out_bias.dtype
        ),
        lax.all_gather(norm_gain.astype(jnp.bfloat16), "fsdp", axis=1, tiled=True).astype(
            norm_gain.dtype
        ),
        lax.all_gather(norm_bias.astype(jnp.bfloat16), "fsdp", axis=1, tiled=True).astype(
            norm_bias.dtype
        ),
    )

    def head_total(partial_value):
        return tp_total(partial_value.astype(jnp.bfloat16))

    inputs = tokens[0]
    resid_in = inputs.astype(jnp.float32)
    query_segs = block_ids[0]
    top_seg = jnp.max(query_segs)
    low_seg = jnp.min(query_segs)
    rows = inputs.shape[0]
    queries = (matmul(inputs, w_qkv[0]) + b_attn[0]).astype(jnp.bfloat16)
    keys = matmul(inputs, w_qkv[1]).astype(jnp.bfloat16)
    values = (matmul(inputs, w_qkv[2]) + b_attn[1]).astype(jnp.bfloat16)
    query_heads = split_heads(queries)
    key_heads = split_heads(keys)
    value_heads = split_heads(values)
    heads = query_heads.shape[1]
    start_state = (jnp.full((rows, heads), NEG, jnp.float32), jnp.zeros((rows, heads), jnp.float32))
    empty_heads = jnp.zeros((rows, heads, HEAD), jnp.float32)

    def over_ctx(x):
        stacked = gather_by_exchange(x, "ctx")
        return stacked.reshape((-1,) + x.shape[1:])

    both = over_ctx(jnp.concatenate([keys, values], axis=1))
    all_keys, all_values = both[:, : keys.shape[1]], both[:, keys.shape[1] :]
    all_segs = over_ctx(query_segs)

    def stat_one_block(inner, block):

        def stat_compute(current):
            row_max, row_sum = current
            scores = scores_of(query_heads, split_heads(block[0]), query_segs, block[1])
            new_max = jnp.maximum(row_max, jnp.max(scores, axis=-1))
            total = row_sum * jnp.exp(row_max - new_max) + jnp.sum(
                jnp.exp(scores - new_max[..., None]), axis=-1
            )
            return (new_max, total)

        return (lax.cond(jnp.min(block[1]) <= top_seg, stat_compute, pass_state, inner), None)

    row_max, row_sum = lax.scan(
        stat_one_block,
        start_state,
        in_blocks(
            (
                all_keys,
                all_segs,
            )
        ),
    )[0]
    log_sum = row_max + jnp.log(row_sum)

    def out_one_block(inner, block):

        def out_compute(current):
            scores = scores_of(query_heads, split_heads(block[0]), query_segs, block[2])
            weights = jnp.exp(scores - log_sum[..., None]).astype(jnp.bfloat16)
            return current + jnp.einsum(
                "qhk,khd->qhd", weights, split_heads(block[1]), preferred_element_type=jnp.float32
            )

        return (lax.cond(jnp.min(block[2]) <= top_seg, out_compute, pass_state, inner), None)

    mixed = lax.scan(
        out_one_block,
        empty_heads,
        in_blocks(
            (
                all_keys,
                all_values,
                all_segs,
            )
        ),
    )[0]
    mixed_low = mixed.reshape(rows, -1).astype(jnp.bfloat16)
    self_branch = head_total(matmul(mixed_low, w_out)) + b_out[0]
    first, first_norm, first_inv = norm_forward(resid_in + self_branch, gains[0], shifts[0])
    first_low = first.astype(jnp.bfloat16)
    states_all = over_ctx(source_states[0])
    cross_query = (matmul(first_low, w_cq) + b_attn[2]).astype(jnp.bfloat16)
    cross_keys = matmul(states_all, w_ckv[0]).astype(jnp.bfloat16)
    cross_values = (matmul(states_all, w_ckv[1]) + b_attn[3]).astype(jnp.bfloat16)
    cq_heads = split_heads(cross_query)
    ck_heads = split_heads(cross_keys)
    cv_heads = split_heads(cross_values)
    reach = jnp.arange(states_all.shape[0]) < source_len[0]
    cross_scores = jnp.einsum(
        "qhd,khd->qhk", cq_heads, ck_heads, preferred_element_type=jnp.float32
    ) * HEAD ** (-0.5)
    cross_scores = jnp.where(reach[None, None, :], cross_scores, NEG)
    cross_top = jnp.max(cross_scores, axis=-1, keepdims=True)
    powers = jnp.exp(cross_scores - cross_top)
    cross_weights = powers / jnp.sum(powers, axis=-1, keepdims=True)
    cross_low = cross_weights.astype(jnp.bfloat16)
    looked = (
        jnp.einsum("qhk,khd->qhd", cross_low, cv_heads, preferred_element_type=jnp.float32)
        .reshape(rows, -1)
        .astype(jnp.bfloat16)
    )
    cross_branch = head_total(matmul(looked, w_co)) + b_out[1]
    second, second_norm, second_inv = norm_forward(first + cross_branch, gains[1], shifts[1])
    second_low = second.astype(jnp.bfloat16)
    hidden = matmul(second_low, w_in) + ffn_in_bias
    sigma = 1.0 / (1.0 + jnp.exp(-hidden))
    active = (hidden / (1.0 + jnp.exp(-hidden))).astype(jnp.bfloat16)
    ffn_branch = head_total(matmul(active, w_fout)) + b_out[2]
    result, third_norm, third_inv = norm_forward(second + ffn_branch, gains[2], shifts[2])
    grad_third, gain_third, shift_third = norm_backward(
        out_grad[0].astype(jnp.float32), third_norm, third_inv, gains[2]
    )
    grad_ffn_low = grad_third.astype(jnp.bfloat16)
    grad_active = matmul_nt(grad_ffn_low, w_fout)
    grad_hidden = (grad_active * sigma * (1.0 + hidden * (1.0 - sigma))).astype(jnp.bfloat16)
    grad_second_in = grad_third + head_total(matmul_nt(grad_hidden, w_in))
    g_fin = matmul_tn(second_low, grad_hidden)
    g_fbias = jnp.sum(grad_hidden.astype(jnp.float32), axis=0)
    g_fout = matmul_tn(active, grad_ffn_low)
    grad_second, gain_second, shift_second = norm_backward(
        grad_second_in, second_norm, second_inv, gains[1]
    )
    grad_cross_low = grad_second.astype(jnp.bfloat16)
    grad_looked = matmul_nt(grad_cross_low, w_co).astype(jnp.bfloat16)
    gl_heads = split_heads(grad_looked)
    grad_cweights = jnp.einsum(
        "qhd,khd->qhk", gl_heads, cv_heads, preferred_element_type=jnp.float32
    )
    grad_cscores = cross_weights * (
        grad_cweights - jnp.sum(cross_weights * grad_cweights, axis=-1, keepdims=True)
    )
    grad_cscores = grad_cscores.astype(jnp.bfloat16)
    grad_cq = (
        (
            jnp.einsum("qhk,khd->qhd", grad_cscores, ck_heads, preferred_element_type=jnp.float32)
            * HEAD ** (-0.5)
        )
        .reshape(rows, -1)
        .astype(jnp.bfloat16)
    )
    part_ck = (
        jnp.einsum("qhk,qhd->khd", grad_cscores, cq_heads, preferred_element_type=jnp.float32)
        * HEAD ** (-0.5)
    ).reshape(states_all.shape[0], -1)
    part_cv = jnp.einsum(
        "qhk,qhd->khd", cross_low, gl_heads, preferred_element_type=jnp.float32
    ).reshape(states_all.shape[0], -1)
    grad_ck, grad_cv = in_one_piece(
        (part_ck.astype(jnp.bfloat16), part_cv.astype(jnp.bfloat16)), "ctx", 0, 1
    )
    grad_ck_low = grad_ck.astype(jnp.bfloat16)
    grad_cv_low = grad_cv.astype(jnp.bfloat16)
    local_states = source_states[0]
    g_ckv = jnp.stack([matmul_tn(local_states, grad_ck_low), matmul_tn(local_states, grad_cv_low)])
    source_part = matmul_nt(grad_ck_low, w_ckv[0]) + matmul_nt(grad_cv_low, w_ckv[1])
    grad_first_in = grad_second + head_total(matmul_nt(grad_cq, w_cq))
    g_cq = matmul_tn(first_low, grad_cq)
    g_co = matmul_tn(looked, grad_cross_low)
    grad_first, gain_first, shift_first = norm_backward(
        grad_first_in, first_norm, first_inv, gains[0]
    )
    grad_self_low = grad_first.astype(jnp.bfloat16)
    grad_mixed = matmul_nt(grad_self_low, w_out).astype(jnp.bfloat16)
    gm_heads = split_heads(grad_mixed)
    delta = jnp.sum(gm_heads.astype(jnp.float32) * mixed, axis=-1)

    def query_one_block(inner, block):

        def query_compute(current):
            block_keys = split_heads(block[0])
            scores = scores_of(query_heads, block_keys, query_segs, block[2])
            probs = jnp.exp(scores - log_sum[..., None])
            grad_probs = jnp.einsum(
                "qhd,khd->qhk", gm_heads, split_heads(block[1]), preferred_element_type=jnp.float32
            )
            grad_scores = (probs * (grad_probs - delta[..., None])).astype(jnp.bfloat16)
            return current + jnp.einsum(
                "qhk,khd->qhd", grad_scores, block_keys, preferred_element_type=jnp.float32
            )

        return (lax.cond(jnp.min(block[2]) <= top_seg, query_compute, pass_state, inner), None)

    grad_q_sum = lax.scan(
        query_one_block,
        empty_heads,
        in_blocks(
            (
                all_keys,
                all_values,
                all_segs,
            )
        ),
    )[0]
    all_log_sum, all_delta = (
        over_ctx(log_sum),
        over_ctx(delta),
    )

    def key_one_block(inner, block):
        remote_q, remote_grad, remote_segs, block_sum, block_delta = block

        def key_compute(current):
            grad_key_sum, grad_value_sum = current
            remote_heads = split_heads(remote_q)
            remote_grads = split_heads(remote_grad)
            scores = scores_of(remote_heads, key_heads, remote_segs, query_segs)
            probs = jnp.exp(scores - block_sum[..., None])
            grad_value_sum = grad_value_sum + jnp.einsum(
                "qhk,qhd->khd",
                probs.astype(jnp.bfloat16),
                remote_grads,
                preferred_element_type=jnp.float32,
            )
            grad_probs = jnp.einsum(
                "qhd,khd->qhk", remote_grads, value_heads, preferred_element_type=jnp.float32
            )
            grad_scores = (probs * (grad_probs - block_delta[..., None])).astype(jnp.bfloat16)
            grad_key_sum = grad_key_sum + jnp.einsum(
                "qhk,qhd->khd", grad_scores, remote_heads, preferred_element_type=jnp.float32
            )
            return (grad_key_sum, grad_value_sum)

        return (lax.cond(jnp.max(remote_segs) >= low_seg, key_compute, pass_state, inner), None)

    grad_k_sum, grad_v_sum = lax.scan(
        key_one_block,
        (empty_heads, empty_heads),
        in_blocks(
            (
                over_ctx(queries),
                over_ctx(grad_mixed),
                all_segs,
            )
            + (all_log_sum, all_delta)
        ),
    )[0]
    grad_q = (grad_q_sum * HEAD ** (-0.5)).reshape(rows, -1).astype(jnp.bfloat16)
    grad_k = (grad_k_sum * HEAD ** (-0.5)).reshape(rows, -1).astype(jnp.bfloat16)
    grad_v = grad_v_sum.reshape(rows, -1).astype(jnp.bfloat16)
    input_part = (
        matmul_nt(grad_q, w_qkv[0]) + matmul_nt(grad_k, w_qkv[1]) + matmul_nt(grad_v, w_qkv[2])
    )
    input_sum, source_sum = (
        tp_total(input_part.astype(jnp.bfloat16)),
        tp_total(source_part.astype(jnp.bfloat16)),
    )
    input_grad = grad_first + input_sum
    g_qkv = jnp.stack(
        [matmul_tn(inputs, grad_q), matmul_tn(inputs, grad_k), matmul_tn(inputs, grad_v)]
    )
    g_out = matmul_tn(mixed_low, grad_self_low)
    g_abias = jnp.stack(
        [
            jnp.sum(grad_q.astype(jnp.float32), axis=0),
            jnp.sum(grad_v.astype(jnp.float32), axis=0),
            jnp.sum(grad_cq.astype(jnp.float32), axis=0),
            jnp.sum(grad_cv_low.astype(jnp.float32), axis=0),
        ]
    )
    g_obias = jnp.stack(
        [jnp.sum(grad_first, axis=0), jnp.sum(grad_second, axis=0), jnp.sum(grad_third, axis=0)]
    )
    g_gain = jnp.stack([gain_first, gain_second, gain_third])
    g_shift = jnp.stack([shift_first, shift_second, shift_third])
    big = (
        (g_qkv, 1),
        (g_out, 1),
        (g_cq, 0),
        (g_ckv, 1),
        (g_co, 1),
        (g_fin, 0),
        (g_fout, 1),
        (g_abias, 0),
        (g_obias, 1),
        (g_gain, 1),
        (g_shift, 1),
    )
    halves = [pair_scatter(g, dim) for g, dim in big]
    flats = [h.astype(jnp.bfloat16).reshape(-1) for h in halves]
    size = lax.axis_size("ctx")
    lengths = [f.shape[0] for f in flats]
    pad = -sum(lengths) % (512 * 16 * size)
    packed = jnp.concatenate(flats + [jnp.zeros((pad,), jnp.bfloat16)]).reshape(-1, 512)
    summed = ctx_total(packed).reshape(-1).astype(jnp.float32)
    outs, at = [], 0
    for h, length in zip(halves, lengths):
        outs.append(summed[at : at + length].reshape(h.shape))
        at += length
    o_qkv, o_out, o_cq, o_ckv, o_co, o_fin, o_fout, o_abias, o_obias, o_gain, o_shift = outs
    squares = jnp.stack(
        [
            jnp.sum(resid_in * resid_in),
            jnp.sum(self_branch * self_branch),
            jnp.sum(cross_branch * cross_branch),
            jnp.sum(ffn_branch * ffn_branch),
        ]
    )
    fbias_total, square_total = lax.psum((g_fbias, squares), ("fsdp", "ctx"))
    entries = rows * inputs.shape[1] * lax.axis_size("fsdp") * lax.axis_size("ctx")
    rms_values = jnp.sqrt(square_total / entries)
    return (
        result[None].astype(jnp.bfloat16),
        input_grad[None],
        source_sum[None],
        rms_values,
        o_qkv,
        o_out,
        o_cq,
        o_ckv,
        o_co,
        o_fin,
        o_fout,
        o_abias,
        fbias_total,
        o_obias,
        o_gain,
        o_shift,
    )


def solution(mesh):
    in_specs = (
        P("fsdp", "ctx", None),
        P("fsdp", "ctx", None),
        P("fsdp", "ctx"),
        P("fsdp"),
        P("fsdp", "ctx", None),
        P(None, "fsdp", "tp"),
        P("tp", "fsdp"),
        P("fsdp", "tp"),
        P(None, "fsdp", "tp"),
        P("tp", "fsdp"),
        P("fsdp", "tp"),
        P("tp", "fsdp"),
        P("fsdp", "tp"),
        P("tp"),
        P(None, "fsdp"),
        P(None, "fsdp"),
        P(None, "fsdp"),
    )
    out_specs = (
        P("fsdp", "ctx", None),
        P("fsdp", "ctx", None),
        P("fsdp", "ctx", None),
        P(),
        P(None, "fsdp", "tp"),
        P("tp", "fsdp"),
        P("fsdp", "tp"),
        P(None, "fsdp", "tp"),
        P("tp", "fsdp"),
        P("fsdp", "tp"),
        P("tp", "fsdp"),
        P("fsdp", "tp"),
        P("tp"),
        P(None, "fsdp"),
        P(None, "fsdp"),
        P(None, "fsdp"),
    )
    return jax.shard_map(
        per_device, mesh=mesh, in_specs=in_specs, out_specs=out_specs, check_vma=False
    )
```

```python
import jax
import jax.numpy as jnp
from jax import lax
from jax.experimental import pallas as pl
from jax.experimental.pallas import tpu as pltpu
from jax.sharding import PartitionSpec as P

HEAD = 64


NEG = -1e30
EPSILON = 1e-05


def cut_along(x, dim, devices):
    before, after = (x.shape[:dim], x.shape[dim + 1 :])
    return jnp.moveaxis(x.reshape(*before, devices, -1, *after), dim, 0)


def sum_at_owner(x, axis, dim):
    pieces = cut_along(x, dim, lax.axis_size(axis))
    arrived = lax.all_to_all(pieces, axis, split_axis=0, concat_axis=0, tiled=True)
    return arrived.astype(jnp.float32).sum(axis=0)


def in_one_piece(arrays, axis, dim, along):
    both = jnp.concatenate(arrays, axis=along)
    out, at, done = (sum_at_owner(both, axis, dim), 0, [])
    for a in arrays:
        done.append(lax.slice_in_dim(out, at, at + a.shape[along], axis=along))
        at += a.shape[along]
    return tuple(done)


def other(axis):
    size = lax.axis_size(axis)
    return [(i, (i + size // 2) % size) for i in range(size)]


def tp_total(part):
    return part.astype(jnp.float32) + lax.ppermute(part, "tp", other("tp")).astype(jnp.float32)


def pair_scatter(x, dim):
    half = x.shape[dim] // 2
    me = lax.axis_index("fsdp")
    sent = lax.dynamic_slice_in_dim(x, (1 - me) * half, half, dim).astype(jnp.bfloat16)
    kept = lax.dynamic_slice_in_dim(x, me * half, half, dim)
    return kept + lax.ppermute(sent, "fsdp", other("fsdp")).astype(jnp.float32)


def gather_by_exchange(x, axis):
    size = lax.axis_size(axis)
    return lax.all_to_all(
        jnp.broadcast_to(x[None], (size,) + x.shape), axis, split_axis=0, concat_axis=0, tiled=True
    )


def ctx_total(x):
    size = lax.axis_size("ctx")
    pieces = x.reshape(size, -1, x.shape[1])
    arrived = lax.all_to_all(pieces, "ctx", split_axis=0, concat_axis=0, tiled=True)
    mine = arrived.astype(jnp.float32).sum(axis=0).astype(jnp.bfloat16)
    return gather_by_exchange(mine, "ctx").reshape(x.shape)


def matmul(left, right):
    return jnp.dot(left, right, preferred_element_type=jnp.float32)


def matmul_tn(left, right):
    return lax.dot_general(
        left, right, (((0,), (0,)), ((), ())), preferred_element_type=jnp.float32
    )


def matmul_nt(left, right):
    return lax.dot_general(
        left, right, (((1,), (1,)), ((), ())), preferred_element_type=jnp.float32
    )


def split_heads(matrix):
    return matrix.reshape(matrix.shape[0], matrix.shape[1] // HEAD, HEAD)


def norm_forward(resid, gain, shift):
    average = jnp.mean(resid, axis=-1, keepdims=True)
    centred = resid - average
    inverse = lax.rsqrt(jnp.mean(centred * centred, axis=-1, keepdims=True) + EPSILON)
    normed = centred * inverse
    return (normed * gain + shift, normed, inverse)


def norm_backward(grad_out, normed, inverse, gain):
    grad_norm = grad_out * gain
    first_mean = jnp.mean(grad_norm, axis=-1, keepdims=True)
    second_mean = jnp.mean(grad_norm * normed, axis=-1, keepdims=True)
    grad_in = inverse * (grad_norm - first_mean - normed * second_mean)
    return (grad_in, jnp.sum(grad_out * normed, axis=0), jnp.sum(grad_out, axis=0))


def pass_state(state):
    return state


def seg_column(rows):
    wide = jnp.broadcast_to(rows[:1].astype(jnp.float32), (128, rows.shape[1]))
    return wide.T[:, :1]


def turned(block):
    return block.astype(jnp.float32).T.astype(jnp.bfloat16)


def attend_kernel(low_ref, high_ref, q_ref, kv_ref, o_ref, stat_ref, key_ref, seg_ref):
    step = pl.program_id(0)
    chunks = kv_ref.shape[0]
    width = kv_ref.shape[2]

    @pl.when(step == 0)
    def _():
        @pl.loop(0, chunks)
        def _(j):
            key_ref[j] = turned(kv_ref[j, :HEAD])
            seg_ref[j] = seg_column(kv_ref[j, 2 * HEAD :])

    queries = (q_ref[0, :HEAD].astype(jnp.float32) * HEAD ** (-0.5)).astype(jnp.bfloat16)
    own_seg = q_ref[0, 3 * HEAD :][:1].astype(jnp.float32)
    top = high_ref[step]

    def one(j, state):
        def compute(state):
            row_max, row_sum, total = state
            scores = matmul(key_ref[j], queries)
            scores = jnp.where(seg_ref[j] <= own_seg, scores, NEG)
            new_max = jnp.maximum(row_max, jnp.max(scores, axis=0, keepdims=True))
            keep = jnp.exp(row_max - new_max)
            powers = jnp.exp(scores - new_max)
            row_sum = row_sum * keep + jnp.sum(powers, axis=0, keepdims=True)
            total = total * keep + matmul(kv_ref[j, HEAD : 2 * HEAD], powers.astype(jnp.bfloat16))
            return (new_max, row_sum, total)

        return lax.cond(low_ref[j] <= top, compute, pass_state, state)

    start = (
        jnp.full((1, width), NEG, jnp.float32),
        jnp.zeros((1, width), jnp.float32),
        jnp.zeros((HEAD, width), jnp.float32),
    )
    row_max, row_sum, total = lax.fori_loop(0, chunks, one, start)
    o_ref[0] = total / row_sum
    stat_ref[0] = row_max + jnp.log(row_sum)


def attend_back_kernel(
    low_ref, high_ref, q_ref, kv_ref, g_ref, o_ref, stat_ref, dq_ref, dkv_ref, key_ref, val_ref, seg_ref
):
    step = pl.program_id(0)
    chunks = kv_ref.shape[0]
    width = kv_ref.shape[2]

    @pl.when(step == 0)
    def _():
        @pl.loop(0, chunks)
        def _(j):
            key_ref[j] = turned(kv_ref[j, :HEAD])
            val_ref[j] = turned(kv_ref[j, HEAD : 2 * HEAD])
            seg_ref[j] = seg_column(kv_ref[j, 2 * HEAD :])
            dkv_ref[j] = jnp.zeros(dkv_ref.shape[1:], jnp.float32)

    queries = (q_ref[0, :HEAD].astype(jnp.float32) * HEAD ** (-0.5)).astype(jnp.bfloat16)
    own_seg = q_ref[0, 3 * HEAD :][:1].astype(jnp.float32)
    grads = g_ref[0]
    delta = jnp.sum(grads.astype(jnp.float32) * o_ref[0], axis=0, keepdims=True)
    log_sum = stat_ref[0]
    top = high_ref[step]

    def one(j, total):
        def compute(total):
            scores = matmul(key_ref[j], queries)
            scores = jnp.where(seg_ref[j] <= own_seg, scores, NEG)
            probs = jnp.exp(scores - log_sum)
            grad_probs = matmul(val_ref[j], grads)
            grad_scores = (probs * (grad_probs - delta)).astype(jnp.bfloat16)
            dkv_ref[j, :HEAD] += matmul_nt(queries, grad_scores)
            dkv_ref[j, HEAD:] += matmul_nt(grads, probs.astype(jnp.bfloat16))
            return total + matmul(kv_ref[j, :HEAD], grad_scores)

        return lax.cond(low_ref[j] <= top, compute, pass_state, total)

    total = lax.fori_loop(0, chunks, one, jnp.zeros((HEAD, width), jnp.float32))
    dq_ref[0] = (total * HEAD ** (-0.5)).astype(jnp.bfloat16)


def whole(shape):
    return pl.BlockSpec(shape, lambda i, *_: (0,) * len(shape))


def by_step(shape):
    return pl.BlockSpec((1,) + shape[1:], lambda i, *_: (i,) + (0,) * (len(shape) - 1))


def attend(low, high, own, kv):
    count, _, width = own.shape
    chunks = kv.shape[0]
    outs = (
        jax.ShapeDtypeStruct((count, HEAD, width), jnp.float32),
        jax.ShapeDtypeStruct((count, 1, width), jnp.float32),
    )
    pairs = count * chunks * width * width
    return pl.pallas_call(
        attend_kernel,
        out_shape=outs,
        grid_spec=pltpu.PrefetchScalarGridSpec(
            num_scalar_prefetch=2,
            grid=(count,),
            in_specs=[by_step(own.shape), whole(kv.shape)],
            out_specs=[by_step(o.shape) for o in outs],
            scratch_shapes=[
                pltpu.VMEM((chunks, width, HEAD), jnp.bfloat16),
                pltpu.VMEM((chunks, width, 1), jnp.float32),
            ],
        ),
        cost_estimate=pl.CostEstimate(
            flops=2 * HEAD * pairs, transcendentals=pairs // 2, bytes_accessed=kv.size * 2
        ),
        name="attend",
    )(low, high, own, kv)


def attend_back(low, high, own, kv, grads, mixed, log_sum):
    count, _, width = own.shape
    chunks = kv.shape[0]
    outs = (
        jax.ShapeDtypeStruct((count, HEAD, width), jnp.bfloat16),
        jax.ShapeDtypeStruct((chunks, 2 * HEAD, width), jnp.float32),
    )
    pairs = count * chunks * width * width
    return pl.pallas_call(
        attend_back_kernel,
        out_shape=outs,
        grid_spec=pltpu.PrefetchScalarGridSpec(
            num_scalar_prefetch=2,
            grid=(count,),
            in_specs=[
                by_step(own.shape),
                whole(kv.shape),
                by_step(grads.shape),
                by_step(mixed.shape),
                by_step(log_sum.shape),
            ],
            out_specs=[by_step(outs[0].shape), whole(outs[1].shape)],
            scratch_shapes=[
                pltpu.VMEM((chunks, width, HEAD), jnp.bfloat16),
                pltpu.VMEM((chunks, width, HEAD), jnp.bfloat16),
                pltpu.VMEM((chunks, width, 1), jnp.float32),
            ],
        ),
        cost_estimate=pl.CostEstimate(
            flops=5 * HEAD * pairs, transcendentals=pairs // 2, bytes_accessed=kv.size * 8
        ),
        name="attend_back",
    )(low, high, own, kv, grads, mixed, log_sum)


def head_groups(heads):
    members = lax.axis_size("ctx") // heads
    return [[head * members + m for head in range(heads)] for m in range(members)]


def to_heads(pieces):
    groups = head_groups(pieces.shape[0])
    return lax.all_to_all(pieces, "ctx", 0, 0, axis_index_groups=groups, tiled=True)


def member_shift(heads, shift):
    size = lax.axis_size("ctx")
    members = size // heads
    return [(i, i // members * members + (i + shift) % members) for i in range(size)]


def per_device(
    tokens,
    source_states,
    block_ids,
    source_len,
    out_grad,
    self_qkv,
    self_out,
    cross_q,
    cross_kv,
    cross_out,
    ffn_in,
    ffn_out,
    attn_bias,
    ffn_in_bias,
    out_bias,
    norm_gain,
    norm_bias,
):
    w_qkv, w_out, w_cq, w_ckv, w_co, w_in, w_fout, b_attn, b_out, gains, shifts = (
        lax.all_gather(self_qkv, "fsdp", axis=1, tiled=True),
        lax.all_gather(self_out, "fsdp", axis=1, tiled=True),
        lax.all_gather(cross_q, "fsdp", axis=0, tiled=True),
        lax.all_gather(cross_kv, "fsdp", axis=1, tiled=True),
        lax.all_gather(cross_out, "fsdp", axis=1, tiled=True),
        lax.all_gather(ffn_in, "fsdp", axis=0, tiled=True),
        lax.all_gather(ffn_out, "fsdp", axis=1, tiled=True),
        lax.all_gather(attn_bias.astype(jnp.bfloat16), "fsdp", axis=0, tiled=True).astype(
            attn_bias.dtype
        ),
        lax.all_gather(out_bias.astype(jnp.bfloat16), "fsdp", axis=1, tiled=True).astype(
            out_bias.dtype
        ),
        lax.all_gather(norm_gain.astype(jnp.bfloat16), "fsdp", axis=1, tiled=True).astype(
            norm_gain.dtype
        ),
        lax.all_gather(norm_bias.astype(jnp.bfloat16), "fsdp", axis=1, tiled=True).astype(
            norm_bias.dtype
        ),
    )

    def head_total(partial_value):
        return tp_total(partial_value.astype(jnp.bfloat16))

    def over_ctx(x):
        stacked = gather_by_exchange(x, "ctx")
        return stacked.reshape((-1,) + x.shape[1:])

    inputs = tokens[0]
    resid_in = inputs.astype(jnp.float32)
    query_segs = block_ids[0]
    rows = inputs.shape[0]
    local_heads = w_qkv.shape[2] // HEAD
    shift_v = jnp.stack([b_attn[0], jnp.zeros_like(b_attn[0]), b_attn[1]])
    packed = lax.dot_general(w_qkv, inputs, (((1,), (1,)), ((), ())), preferred_element_type=jnp.float32)
    packed = (packed + shift_v[:, :, None]).astype(jnp.bfloat16)
    packed = packed.reshape(3, local_heads, HEAD, rows).swapaxes(0, 1)
    packed = packed.reshape(local_heads, 3 * HEAD, rows)
    seg_rows = jnp.broadcast_to(query_segs.astype(jnp.bfloat16), (local_heads, 16, rows))
    own = to_heads(jnp.concatenate([packed, seg_rows], axis=1))
    members = lax.axis_size("ctx") // local_heads
    rounds = tuple(range(1, members))
    own_kv = own[:, HEAD:]
    kv = jnp.concatenate(
        [own_kv] + [lax.ppermute(own_kv, "ctx", member_shift(local_heads, -s)) for s in rounds]
    )
    low = kv[:, 2 * HEAD, 0].astype(jnp.int32)
    high = kv[:local_heads, 2 * HEAD, rows - 1].astype(jnp.int32)
    head_out, log_sum = attend(low, high, own, kv)
    mixed_t = to_heads(head_out.astype(jnp.bfloat16)).reshape(-1, rows)
    mixed_low = mixed_t.T
    self_branch = head_total(matmul(mixed_low, w_out)) + b_out[0]
    first, first_norm, first_inv = norm_forward(resid_in + self_branch, gains[0], shifts[0])
    first_low = first.astype(jnp.bfloat16)
    states_all = over_ctx(source_states[0])
    cross_query = (matmul(first_low, w_cq) + b_attn[2]).astype(jnp.bfloat16)
    cross_keys = matmul(states_all, w_ckv[0]).astype(jnp.bfloat16)
    cross_values = (matmul(states_all, w_ckv[1]) + b_attn[3]).astype(jnp.bfloat16)
    cq_heads = split_heads(cross_query)
    ck_heads = split_heads(cross_keys)
    cv_heads = split_heads(cross_values)
    reach = jnp.arange(states_all.shape[0]) < source_len[0]
    cross_scores = jnp.einsum(
        "qhd,khd->qhk", cq_heads, ck_heads, preferred_element_type=jnp.float32
    ) * HEAD ** (-0.5)
    cross_scores = jnp.where(reach[None, None, :], cross_scores, NEG)
    cross_top = jnp.max(cross_scores, axis=-1, keepdims=True)
    powers = jnp.exp(cross_scores - cross_top)
    cross_weights = powers / jnp.sum(powers, axis=-1, keepdims=True)
    cross_low = cross_weights.astype(jnp.bfloat16)
    looked = (
        jnp.einsum("qhk,khd->qhd", cross_low, cv_heads, preferred_element_type=jnp.float32)
        .reshape(rows, -1)
        .astype(jnp.bfloat16)
    )
    cross_branch = head_total(matmul(looked, w_co)) + b_out[1]
    second, second_norm, second_inv = norm_forward(first + cross_branch, gains[1], shifts[1])
    second_low = second.astype(jnp.bfloat16)
    hidden = matmul(second_low, w_in) + ffn_in_bias
    sigma = 1.0 / (1.0 + jnp.exp(-hidden))
    active = (hidden / (1.0 + jnp.exp(-hidden))).astype(jnp.bfloat16)
    ffn_branch = head_total(matmul(active, w_fout)) + b_out[2]
    result, third_norm, third_inv = norm_forward(second + ffn_branch, gains[2], shifts[2])
    grad_third, gain_third, shift_third = norm_backward(
        out_grad[0].astype(jnp.float32), third_norm, third_inv, gains[2]
    )
    grad_ffn_low = grad_third.astype(jnp.bfloat16)
    grad_active = matmul_nt(grad_ffn_low, w_fout)
    grad_hidden = (grad_active * sigma * (1.0 + hidden * (1.0 - sigma))).astype(jnp.bfloat16)
    grad_second_in = grad_third + head_total(matmul_nt(grad_hidden, w_in))
    g_fin = matmul_tn(second_low, grad_hidden)
    g_fbias = jnp.sum(grad_hidden.astype(jnp.float32), axis=0)
    g_fout = matmul_tn(active, grad_ffn_low)
    grad_second, gain_second, shift_second = norm_backward(
        grad_second_in, second_norm, second_inv, gains[1]
    )
    grad_cross_low = grad_second.astype(jnp.bfloat16)
    grad_looked = matmul_nt(grad_cross_low, w_co).astype(jnp.bfloat16)
    gl_heads = split_heads(grad_looked)
    grad_cweights = jnp.einsum(
        "qhd,khd->qhk", gl_heads, cv_heads, preferred_element_type=jnp.float32
    )
    grad_cscores = cross_weights * (
        grad_cweights - jnp.sum(cross_weights * grad_cweights, axis=-1, keepdims=True)
    )
    grad_cscores = grad_cscores.astype(jnp.bfloat16)
    grad_cq = (
        (
            jnp.einsum("qhk,khd->qhd", grad_cscores, ck_heads, preferred_element_type=jnp.float32)
            * HEAD ** (-0.5)
        )
        .reshape(rows, -1)
        .astype(jnp.bfloat16)
    )
    part_ck = (
        jnp.einsum("qhk,qhd->khd", grad_cscores, cq_heads, preferred_element_type=jnp.float32)
        * HEAD ** (-0.5)
    ).reshape(states_all.shape[0], -1)
    part_cv = jnp.einsum(
        "qhk,qhd->khd", cross_low, gl_heads, preferred_element_type=jnp.float32
    ).reshape(states_all.shape[0], -1)
    grad_ck, grad_cv = in_one_piece(
        (part_ck.astype(jnp.bfloat16), part_cv.astype(jnp.bfloat16)), "ctx", 0, 1
    )
    grad_ck_low = grad_ck.astype(jnp.bfloat16)
    grad_cv_low = grad_cv.astype(jnp.bfloat16)
    local_states = source_states[0]
    g_ckv = jnp.stack([matmul_tn(local_states, grad_ck_low), matmul_tn(local_states, grad_cv_low)])
    source_part = matmul_nt(grad_ck_low, w_ckv[0]) + matmul_nt(grad_cv_low, w_ckv[1])
    grad_first_in = grad_second + head_total(matmul_nt(grad_cq, w_cq))
    g_cq = matmul_tn(first_low, grad_cq)
    g_co = matmul_tn(looked, grad_cross_low)
    grad_first, gain_first, shift_first = norm_backward(
        grad_first_in, first_norm, first_inv, gains[0]
    )
    grad_self_low = grad_first.astype(jnp.bfloat16)
    grad_mixed = matmul_nt(grad_self_low, w_out).astype(jnp.bfloat16)
    grads_in = to_heads(grad_mixed.T.reshape(local_heads, HEAD, rows))
    part_q, part_kv = attend_back(low, high, own, kv, grads_in, head_out, log_sum)
    sum_kv = part_kv[:local_heads]
    for s in rounds:
        away = part_kv[s * local_heads : (s + 1) * local_heads].astype(jnp.bfloat16)
        sum_kv = sum_kv + lax.ppermute(away, "ctx", member_shift(local_heads, s)).astype(jnp.float32)
    back = to_heads(jnp.concatenate([part_q, sum_kv.astype(jnp.bfloat16)], axis=1))
    back = back.reshape(local_heads, 3, HEAD, rows).swapaxes(0, 1).reshape(3, -1, rows)
    grad_q, grad_k, grad_v = back[0].T, back[1].T, back[2].T
    input_part = (
        matmul_nt(grad_q, w_qkv[0]) + matmul_nt(grad_k, w_qkv[1]) + matmul_nt(grad_v, w_qkv[2])
    )
    input_sum, source_sum = (
        tp_total(input_part.astype(jnp.bfloat16)),
        tp_total(source_part.astype(jnp.bfloat16)),
    )
    input_grad = grad_first + input_sum
    g_qkv = jnp.stack(
        [matmul_tn(inputs, grad_q), matmul_tn(inputs, grad_k), matmul_tn(inputs, grad_v)]
    )
    g_out = matmul_tn(mixed_low, grad_self_low)
    g_abias = jnp.stack(
        [
            jnp.sum(grad_q.astype(jnp.float32), axis=0),
            jnp.sum(grad_v.astype(jnp.float32), axis=0),
            jnp.sum(grad_cq.astype(jnp.float32), axis=0),
            jnp.sum(grad_cv_low.astype(jnp.float32), axis=0),
        ]
    )
    g_obias = jnp.stack(
        [jnp.sum(grad_first, axis=0), jnp.sum(grad_second, axis=0), jnp.sum(grad_third, axis=0)]
    )
    g_gain = jnp.stack([gain_first, gain_second, gain_third])
    g_shift = jnp.stack([shift_first, shift_second, shift_third])
    big = (
        (g_qkv, 1),
        (g_out, 1),
        (g_cq, 0),
        (g_ckv, 1),
        (g_co, 1),
        (g_fin, 0),
        (g_fout, 1),
        (g_abias, 0),
        (g_obias, 1),
        (g_gain, 1),
        (g_shift, 1),
    )
    squares = jnp.stack(
        [
            jnp.sum(resid_in * resid_in),
            jnp.sum(self_branch * self_branch),
            jnp.sum(cross_branch * cross_branch),
            jnp.sum(ffn_branch * ffn_branch),
        ]
    )
    square_high = squares.astype(jnp.bfloat16)
    square_low = (squares - square_high.astype(jnp.float32)).astype(jnp.bfloat16)
    extra = jnp.concatenate([g_fbias.astype(jnp.bfloat16), square_high, square_low])
    halves = [pair_scatter(g, dim) for g, dim in big]
    flats = [h.astype(jnp.bfloat16).reshape(-1) for h in halves]
    size = lax.axis_size("ctx")
    flats.append(extra)
    lengths = [f.shape[0] for f in flats]
    pad = -sum(lengths) % (512 * 16 * size)
    packed = jnp.concatenate(flats + [jnp.zeros((pad,), jnp.bfloat16)]).reshape(-1, 512)
    summed = ctx_total(packed).reshape(-1).astype(jnp.float32)
    outs, at = [], 0
    for h, length in zip(halves, lengths):
        outs.append(summed[at : at + length].reshape(h.shape))
        at += length
    o_qkv, o_out, o_cq, o_ckv, o_co, o_fin, o_fout, o_abias, o_obias, o_gain, o_shift = outs
    extra_sum = summed[at : at + lengths[-1]]
    extra_sum = extra_sum + lax.ppermute(extra_sum, "fsdp", other("fsdp"))
    fbias_total = extra_sum[:-8]
    square_total = extra_sum[-8:-4] + extra_sum[-4:]
    entries = rows * inputs.shape[1] * lax.axis_size("fsdp") * lax.axis_size("ctx")
    rms_values = jnp.sqrt(square_total / entries)
    return (
        result[None].astype(jnp.bfloat16),
        input_grad[None],
        source_sum[None],
        rms_values,
        o_qkv,
        o_out,
        o_cq,
        o_ckv,
        o_co,
        o_fin,
        o_fout,
        o_abias,
        fbias_total,
        o_obias,
        o_gain,
        o_shift,
    )


def solution(mesh):
    in_specs = (
        P("fsdp", "ctx", None),
        P("fsdp", "ctx", None),
        P("fsdp", "ctx"),
        P("fsdp"),
        P("fsdp", "ctx", None),
        P(None, "fsdp", "tp"),
        P("tp", "fsdp"),
        P("fsdp", "tp"),
        P(None, "fsdp", "tp"),
        P("tp", "fsdp"),
        P("fsdp", "tp"),
        P("tp", "fsdp"),
        P("fsdp", "tp"),
        P("tp"),
        P(None, "fsdp"),
        P(None, "fsdp"),
        P(None, "fsdp"),
    )
    out_specs = (
        P("fsdp", "ctx", None),
        P("fsdp", "ctx", None),
        P("fsdp", "ctx", None),
        P(),
        P(None, "fsdp", "tp"),
        P("tp", "fsdp"),
        P("fsdp", "tp"),
        P(None, "fsdp", "tp"),
        P("tp", "fsdp"),
        P("fsdp", "tp"),
        P("tp", "fsdp"),
        P("fsdp", "tp"),
        P("tp"),
        P(None, "fsdp"),
        P(None, "fsdp"),
        P(None, "fsdp"),
    )
    return jax.shard_map(
        per_device, mesh=mesh, in_specs=in_specs, out_specs=out_specs, check_vma=False
    )
```

```python
import jax
import jax.numpy as jnp
from jax import lax
from jax.experimental import pallas as pl
from jax.experimental.pallas import tpu as pltpu
from jax.sharding import PartitionSpec as P

HEAD = 64


NEG = -1e30
EPSILON = 1e-05


def cut_along(x, dim, devices):
    before, after = (x.shape[:dim], x.shape[dim + 1 :])
    return jnp.moveaxis(x.reshape(*before, devices, -1, *after), dim, 0)


def sum_at_owner(x, axis, dim):
    pieces = cut_along(x, dim, lax.axis_size(axis))
    arrived = lax.all_to_all(pieces, axis, split_axis=0, concat_axis=0, tiled=True)
    return arrived.astype(jnp.float32).sum(axis=0)


def in_one_piece(arrays, axis, dim, along):
    both = jnp.concatenate(arrays, axis=along)
    out, at, done = (sum_at_owner(both, axis, dim), 0, [])
    for a in arrays:
        done.append(lax.slice_in_dim(out, at, at + a.shape[along], axis=along))
        at += a.shape[along]
    return tuple(done)


def other(axis):
    size = lax.axis_size(axis)
    return [(i, (i + size // 2) % size) for i in range(size)]


def tp_total(part):
    return part.astype(jnp.float32) + lax.ppermute(part, "tp", other("tp")).astype(jnp.float32)


def scattered(pairs, own_rows, other_rows, flipped=False):
    half = pairs[0][1].shape[1] // 2
    product = matmul if flipped else matmul_tn
    sent = [product(a, b[:, half:]).astype(jnp.bfloat16) for a, b in pairs]
    sent += [r.astype(jnp.bfloat16) for r in other_rows]
    kept = [product(a, b[:, :half]) for a, b in pairs] + list(own_rows)
    size = lax.axis_size("ctx")
    total = sum(k.shape[0] for k in kept)
    pad = -total % (16 * size)
    arrived = lax.ppermute(jnp.concatenate(sent), "fsdp", other("fsdp"))
    done, at = [], 0
    for k in kept:
        piece = arrived[at : at + k.shape[0]].astype(jnp.float32)
        done.append((k + piece).astype(jnp.bfloat16))
        at += k.shape[0]
    if pad:
        done.append(jnp.zeros((pad, half), jnp.bfloat16))
    return jnp.concatenate(done)


def gather_by_exchange(x, axis):
    size = lax.axis_size(axis)
    return lax.all_to_all(
        jnp.broadcast_to(x[None], (size,) + x.shape), axis, split_axis=0, concat_axis=0, tiled=True
    )


def ctx_total(x):
    size = lax.axis_size("ctx")
    pieces = x.reshape(size, -1, x.shape[1])
    arrived = lax.all_to_all(pieces, "ctx", split_axis=0, concat_axis=0, tiled=True)
    mine = arrived.astype(jnp.float32).sum(axis=0).astype(jnp.bfloat16)
    return gather_by_exchange(mine, "ctx").reshape(x.shape)


def matmul(left, right):
    return jnp.dot(left, right, preferred_element_type=jnp.float32)


def matmul_tn(left, right):
    return lax.dot_general(
        left, right, (((0,), (0,)), ((), ())), preferred_element_type=jnp.float32
    )


def matmul_nt(left, right):
    return lax.dot_general(
        left, right, (((1,), (1,)), ((), ())), preferred_element_type=jnp.float32
    )


def split_heads(matrix):
    return matrix.reshape(matrix.shape[0], matrix.shape[1] // HEAD, HEAD)


def norm_forward(resid, gain, shift):
    average = jnp.mean(resid, axis=-1, keepdims=True)
    centred = resid - average
    inverse = lax.rsqrt(jnp.mean(centred * centred, axis=-1, keepdims=True) + EPSILON)
    normed = centred * inverse
    return (normed * gain + shift, normed, inverse)


def norm_backward(grad_out, normed, inverse, gain):
    grad_norm = grad_out * gain
    first_mean = jnp.mean(grad_norm, axis=-1, keepdims=True)
    second_mean = jnp.mean(grad_norm * normed, axis=-1, keepdims=True)
    grad_in = inverse * (grad_norm - first_mean - normed * second_mean)
    return (grad_in, jnp.sum(grad_out * normed, axis=0), jnp.sum(grad_out, axis=0))


def pass_state(state):
    return state


def seg_column(rows):
    wide = jnp.broadcast_to(rows[:1].astype(jnp.float32), (128, rows.shape[1]))
    return wide.T[:, :1]


def turned(block):
    return block.astype(jnp.float32).T.astype(jnp.bfloat16)


def attend_kernel(low_ref, high_ref, q_ref, kv_ref, o_ref, stat_ref, key_ref, seg_ref):
    step = pl.program_id(0)
    chunks = kv_ref.shape[0]
    width = kv_ref.shape[2]

    @pl.when(step == 0)
    def _():
        @pl.loop(0, chunks)
        def _(j):
            key_ref[j] = turned(kv_ref[j, :HEAD])
            seg_ref[j] = seg_column(kv_ref[j, 2 * HEAD :])

    queries = (q_ref[0, :HEAD].astype(jnp.float32) * HEAD ** (-0.5)).astype(jnp.bfloat16)
    own_seg = q_ref[0, 3 * HEAD :][:1].astype(jnp.float32)
    top = high_ref[step]

    def one(j, state):
        def compute(state):
            row_max, row_sum, total = state
            scores = matmul(key_ref[j], queries)
            scores = jnp.where(seg_ref[j] <= own_seg, scores, NEG)
            new_max = jnp.maximum(row_max, jnp.max(scores, axis=0, keepdims=True))
            keep = jnp.exp(row_max - new_max)
            powers = jnp.exp(scores - new_max)
            row_sum = row_sum * keep + jnp.sum(powers, axis=0, keepdims=True)
            total = total * keep + matmul(kv_ref[j, HEAD : 2 * HEAD], powers.astype(jnp.bfloat16))
            return (new_max, row_sum, total)

        return lax.cond(low_ref[j] <= top, compute, pass_state, state)

    start = (
        jnp.full((1, width), NEG, jnp.float32),
        jnp.zeros((1, width), jnp.float32),
        jnp.zeros((HEAD, width), jnp.float32),
    )
    row_max, row_sum, total = lax.fori_loop(0, chunks, one, start)
    o_ref[0] = total / row_sum
    stat_ref[0] = row_max + jnp.log(row_sum)


def attend_back_kernel(
    low_ref, high_ref, q_ref, kv_ref, g_ref, o_ref, stat_ref, dq_ref, dkv_ref, key_ref, val_ref, seg_ref
):
    step = pl.program_id(0)
    chunks = kv_ref.shape[0]
    width = kv_ref.shape[2]

    @pl.when(step == 0)
    def _():
        @pl.loop(0, chunks)
        def _(j):
            key_ref[j] = turned(kv_ref[j, :HEAD])
            val_ref[j] = turned(kv_ref[j, HEAD : 2 * HEAD])
            seg_ref[j] = seg_column(kv_ref[j, 2 * HEAD :])
            dkv_ref[j] = jnp.zeros(dkv_ref.shape[1:], jnp.float32)

    queries = (q_ref[0, :HEAD].astype(jnp.float32) * HEAD ** (-0.5)).astype(jnp.bfloat16)
    own_seg = q_ref[0, 3 * HEAD :][:1].astype(jnp.float32)
    grads = g_ref[0]
    delta = jnp.sum(grads.astype(jnp.float32) * o_ref[0], axis=0, keepdims=True)
    log_sum = stat_ref[0]
    top = high_ref[step]

    def one(j, total):
        def compute(total):
            scores = matmul(key_ref[j], queries)
            scores = jnp.where(seg_ref[j] <= own_seg, scores, NEG)
            probs = jnp.exp(scores - log_sum)
            grad_probs = matmul(val_ref[j], grads)
            grad_scores = (probs * (grad_probs - delta)).astype(jnp.bfloat16)
            dkv_ref[j, :HEAD] += matmul_nt(queries, grad_scores)
            dkv_ref[j, HEAD:] += matmul_nt(grads, probs.astype(jnp.bfloat16))
            return total + matmul(kv_ref[j, :HEAD], grad_scores)

        return lax.cond(low_ref[j] <= top, compute, pass_state, total)

    total = lax.fori_loop(0, chunks, one, jnp.zeros((HEAD, width), jnp.float32))
    dq_ref[0] = (total * HEAD ** (-0.5)).astype(jnp.bfloat16)


def whole(shape):
    return pl.BlockSpec(shape, lambda i, *_: (0,) * len(shape))


def by_step(shape):
    return pl.BlockSpec((1,) + shape[1:], lambda i, *_: (i,) + (0,) * (len(shape) - 1))


def attend(low, high, own, kv):
    count, _, width = own.shape
    chunks = kv.shape[0]
    outs = (
        jax.ShapeDtypeStruct((count, HEAD, width), jnp.float32),
        jax.ShapeDtypeStruct((count, 1, width), jnp.float32),
    )
    pairs = count * chunks * width * width
    return pl.pallas_call(
        attend_kernel,
        out_shape=outs,
        grid_spec=pltpu.PrefetchScalarGridSpec(
            num_scalar_prefetch=2,
            grid=(count,),
            in_specs=[by_step(own.shape), whole(kv.shape)],
            out_specs=[by_step(o.shape) for o in outs],
            scratch_shapes=[
                pltpu.VMEM((chunks, width, HEAD), jnp.bfloat16),
                pltpu.VMEM((chunks, width, 1), jnp.float32),
            ],
        ),
        cost_estimate=pl.CostEstimate(
            flops=2 * HEAD * pairs, transcendentals=pairs // 2, bytes_accessed=kv.size * 2
        ),
        name="attend",
    )(low, high, own, kv)


def attend_back(low, high, own, kv, grads, mixed, log_sum):
    count, _, width = own.shape
    chunks = kv.shape[0]
    outs = (
        jax.ShapeDtypeStruct((count, HEAD, width), jnp.bfloat16),
        jax.ShapeDtypeStruct((chunks, 2 * HEAD, width), jnp.float32),
    )
    pairs = count * chunks * width * width
    return pl.pallas_call(
        attend_back_kernel,
        out_shape=outs,
        grid_spec=pltpu.PrefetchScalarGridSpec(
            num_scalar_prefetch=2,
            grid=(count,),
            in_specs=[
                by_step(own.shape),
                whole(kv.shape),
                by_step(grads.shape),
                by_step(mixed.shape),
                by_step(log_sum.shape),
            ],
            out_specs=[by_step(outs[0].shape), whole(outs[1].shape)],
            scratch_shapes=[
                pltpu.VMEM((chunks, width, HEAD), jnp.bfloat16),
                pltpu.VMEM((chunks, width, HEAD), jnp.bfloat16),
                pltpu.VMEM((chunks, width, 1), jnp.float32),
            ],
        ),
        cost_estimate=pl.CostEstimate(
            flops=5 * HEAD * pairs, transcendentals=pairs // 2, bytes_accessed=kv.size * 8
        ),
        name="attend_back",
    )(low, high, own, kv, grads, mixed, log_sum)


def head_groups(heads):
    members = lax.axis_size("ctx") // heads
    return [[head * members + m for head in range(heads)] for m in range(members)]


def to_heads(pieces):
    groups = head_groups(pieces.shape[0])
    return lax.all_to_all(pieces, "ctx", 0, 0, axis_index_groups=groups, tiled=True)


def member_shift(heads, shift):
    size = lax.axis_size("ctx")
    members = size // heads
    return [(i, i // members * members + (i + shift) % members) for i in range(size)]


def per_device(
    tokens,
    source_states,
    block_ids,
    source_len,
    out_grad,
    self_qkv,
    self_out,
    cross_q,
    cross_kv,
    cross_out,
    ffn_in,
    ffn_out,
    attn_bias,
    ffn_in_bias,
    out_bias,
    norm_gain,
    norm_bias,
):
    me = lax.axis_index("fsdp")
    half = norm_gain.shape[1]

    def swapped(x):
        return jnp.where(me == 0, x, jnp.roll(x, half, axis=-1))

    def with_other(x, dim):
        return jnp.concatenate([x, lax.ppermute(x, "fsdp", other("fsdp"))], axis=dim)

    w_qkv = with_other(self_qkv, 1)
    small = jnp.concatenate([attn_bias, out_bias, norm_gain, norm_bias])
    small_other = lax.ppermute(small, "fsdp", other("fsdp"))
    small_both = jnp.concatenate([small, small_other], axis=1)
    b_attn = jnp.where(
        me == 0,
        jnp.concatenate([attn_bias, small_other[:2]]),
        jnp.concatenate([small_other[:2], attn_bias]),
    )
    b_out, gains, shifts = small_both[2:5], small_both[5:8], small_both[8:11]
    w_out, w_cq, w_ckv, w_co, w_in, w_fout = (
        with_other(self_out, 1),
        with_other(cross_q, 0),
        with_other(cross_kv, 1),
        with_other(cross_out, 1),
        with_other(ffn_in, 0),
        with_other(ffn_out, 1),
    )

    def head_total(partial_value):
        return tp_total(partial_value.astype(jnp.bfloat16))

    def over_ctx(x):
        stacked = gather_by_exchange(x, "ctx")
        return stacked.reshape((-1,) + x.shape[1:])

    inputs = swapped(tokens[0])
    states_own = swapped(source_states[0])
    resid_in = inputs.astype(jnp.float32)
    query_segs = block_ids[0]
    rows = inputs.shape[0]
    local_heads = w_qkv.shape[2] // HEAD
    shift_v = jnp.stack([b_attn[0], jnp.zeros_like(b_attn[0]), b_attn[1]])
    packed = lax.dot_general(w_qkv, inputs, (((1,), (1,)), ((), ())), preferred_element_type=jnp.float32)
    packed = (packed + shift_v[:, :, None]).astype(jnp.bfloat16)
    packed = packed.reshape(3, local_heads, HEAD, rows).swapaxes(0, 1)
    packed = packed.reshape(local_heads, 3 * HEAD, rows)
    states_all = over_ctx(states_own)
    seg_rows = jnp.broadcast_to(query_segs.astype(jnp.bfloat16), (local_heads, 16, rows))
    own = to_heads(jnp.concatenate([packed, seg_rows], axis=1))
    members = lax.axis_size("ctx") // local_heads
    rounds = tuple(range(1, members))
    own_kv = own[:, HEAD:]
    kv = jnp.concatenate(
        [own_kv] + [lax.ppermute(own_kv, "ctx", member_shift(local_heads, -s)) for s in rounds]
    )
    low = kv[:, 2 * HEAD, 0].astype(jnp.int32)
    high = kv[:local_heads, 2 * HEAD, rows - 1].astype(jnp.int32)
    head_out, log_sum = attend(low, high, own, kv)
    head_out, states_all = lax.optimization_barrier((head_out, states_all))
    mixed_t = to_heads(head_out.astype(jnp.bfloat16)).reshape(-1, rows)
    mixed_low = mixed_t.T
    self_branch = head_total(matmul(mixed_low, w_out)) + b_out[0]
    first, first_norm, first_inv = norm_forward(resid_in + self_branch, gains[0], shifts[0])
    first_low = first.astype(jnp.bfloat16)
    cross_query = (matmul(first_low, w_cq) + b_attn[2]).astype(jnp.bfloat16)
    cross_keys = matmul(states_all, w_ckv[0]).astype(jnp.bfloat16)
    cross_values = (matmul(states_all, w_ckv[1]) + b_attn[3]).astype(jnp.bfloat16)
    cq_heads = split_heads(cross_query)
    ck_heads = split_heads(cross_keys)
    cv_heads = split_heads(cross_values)
    reach = jnp.arange(states_all.shape[0]) < source_len[0]
    cross_scores = jnp.einsum(
        "qhd,khd->qhk", cq_heads, ck_heads, preferred_element_type=jnp.float32
    ) * HEAD ** (-0.5)
    cross_scores = jnp.where(reach[None, None, :], cross_scores, NEG)
    cross_top = jnp.max(cross_scores, axis=-1, keepdims=True)
    powers = jnp.exp(cross_scores - cross_top)
    cross_weights = powers / jnp.sum(powers, axis=-1, keepdims=True)
    cross_low = cross_weights.astype(jnp.bfloat16)
    looked = (
        jnp.einsum("qhk,khd->qhd", cross_low, cv_heads, preferred_element_type=jnp.float32)
        .reshape(rows, -1)
        .astype(jnp.bfloat16)
    )
    cross_branch = head_total(matmul(looked, w_co)) + b_out[1]
    second, second_norm, second_inv = norm_forward(first + cross_branch, gains[1], shifts[1])
    second_low = second.astype(jnp.bfloat16)
    hidden = matmul(second_low, w_in) + ffn_in_bias
    sigma = 1.0 / (1.0 + jnp.exp(-hidden))
    active = (hidden / (1.0 + jnp.exp(-hidden))).astype(jnp.bfloat16)
    ffn_branch = head_total(matmul(active, w_fout)) + b_out[2]
    result, third_norm, third_inv = norm_forward(second + ffn_branch, gains[2], shifts[2])
    grad_third, gain_third, shift_third = norm_backward(
        swapped(out_grad[0]).astype(jnp.float32), third_norm, third_inv, gains[2]
    )
    grad_ffn_low = grad_third.astype(jnp.bfloat16)
    grad_active = matmul_nt(grad_ffn_low, w_fout)
    grad_hidden = (grad_active * sigma * (1.0 + hidden * (1.0 - sigma))).astype(jnp.bfloat16)
    grad_second_in = grad_third + head_total(matmul_nt(grad_hidden, w_in))
    g_fbias = jnp.sum(grad_hidden.astype(jnp.float32), axis=0)
    ffn_sum = ctx_total(
        scattered(((grad_hidden, second_low), (active, grad_ffn_low)), (), ())
    )
    grad_second, gain_second, shift_second = norm_backward(
        grad_second_in, second_norm, second_inv, gains[1]
    )
    grad_cross_low = grad_second.astype(jnp.bfloat16)
    grad_looked = matmul_nt(grad_cross_low, w_co).astype(jnp.bfloat16)
    gl_heads = split_heads(grad_looked)
    grad_cweights = jnp.einsum(
        "qhd,khd->qhk", gl_heads, cv_heads, preferred_element_type=jnp.float32
    )
    grad_cscores = cross_weights * (
        grad_cweights - jnp.sum(cross_weights * grad_cweights, axis=-1, keepdims=True)
    )
    grad_cscores = grad_cscores.astype(jnp.bfloat16)
    grad_cq = (
        (
            jnp.einsum("qhk,khd->qhd", grad_cscores, ck_heads, preferred_element_type=jnp.float32)
            * HEAD ** (-0.5)
        )
        .reshape(rows, -1)
        .astype(jnp.bfloat16)
    )
    part_ck = (
        jnp.einsum("qhk,qhd->khd", grad_cscores, cq_heads, preferred_element_type=jnp.float32)
        * HEAD ** (-0.5)
    ).reshape(states_all.shape[0], -1)
    part_cv = jnp.einsum(
        "qhk,qhd->khd", cross_low, gl_heads, preferred_element_type=jnp.float32
    ).reshape(states_all.shape[0], -1)
    grad_ck, grad_cv = in_one_piece(
        (part_ck.astype(jnp.bfloat16), part_cv.astype(jnp.bfloat16)), "ctx", 0, 1
    )
    grad_ck_low = grad_ck.astype(jnp.bfloat16)
    grad_cv_low = grad_cv.astype(jnp.bfloat16)
    source_part = matmul_nt(grad_ck_low, w_ckv[0]) + matmul_nt(grad_cv_low, w_ckv[1])
    grad_first_in = grad_second + head_total(matmul_nt(grad_cq, w_cq))
    grad_first, gain_first, shift_first = norm_backward(
        grad_first_in, first_norm, first_inv, gains[0]
    )
    grad_self_low = grad_first.astype(jnp.bfloat16)
    middle_sum = ctx_total(
        scattered(
            (
                (mixed_low, grad_self_low),
                (grad_cq, first_low),
                (grad_ck_low, states_own),
                (grad_cv_low, states_own),
                (looked, grad_cross_low),
            ),
            (),
            (),
        )
    )
    grad_mixed = matmul_nt(grad_self_low, w_out).astype(jnp.bfloat16)
    grads_in = to_heads(grad_mixed.T.reshape(local_heads, HEAD, rows))
    part_q, part_kv = attend_back(low, high, own, kv, grads_in, head_out, log_sum)
    sum_kv = part_kv[:local_heads]
    for s in rounds:
        away = part_kv[s * local_heads : (s + 1) * local_heads].astype(jnp.bfloat16)
        sum_kv = sum_kv + lax.ppermute(away, "ctx", member_shift(local_heads, s)).astype(jnp.float32)
    back = to_heads(jnp.concatenate([part_q, sum_kv.astype(jnp.bfloat16)], axis=1))
    back = back.reshape(local_heads, 3, HEAD, rows).swapaxes(0, 1).reshape(3, -1, rows)
    grad_q, grad_k, grad_v = back[0].T, back[1].T, back[2].T
    input_part = (
        matmul_nt(grad_q, w_qkv[0]) + matmul_nt(grad_k, w_qkv[1]) + matmul_nt(grad_v, w_qkv[2])
    )
    input_sum, source_sum = (
        tp_total(input_part.astype(jnp.bfloat16)),
        tp_total(source_part.astype(jnp.bfloat16)),
    )
    input_grad = grad_first + input_sum
    squares = jnp.stack(
        [
            jnp.sum(resid_in * resid_in),
            jnp.sum(self_branch * self_branch),
            jnp.sum(cross_branch * cross_branch),
            jnp.sum(ffn_branch * ffn_branch),
        ]
    )
    square_high = squares.astype(jnp.bfloat16).astype(jnp.float32)
    square_row = jnp.concatenate(
        [square_high, squares - square_high, jnp.zeros((half - 8,), jnp.float32)]
    )[None]
    feature_rows = jnp.stack(
        [
            jnp.sum(grad_first, axis=0),
            jnp.sum(grad_second, axis=0),
            jnp.sum(grad_third, axis=0),
            gain_first,
            gain_second,
            gain_third,
            shift_first,
            shift_second,
            shift_third,
        ]
    )
    self_rows = jnp.stack(
        [jnp.sum(grad_q.astype(jnp.float32), axis=0), jnp.sum(grad_v.astype(jnp.float32), axis=0)]
    )
    cross_rows = jnp.stack(
        [
            jnp.sum(grad_cq.astype(jnp.float32), axis=0),
            jnp.sum(grad_cv_low.astype(jnp.float32), axis=0),
        ]
    )
    common = jnp.concatenate([g_fbias.reshape(-1, half), square_row])
    tail = scattered(
        ((back.reshape(-1, rows), inputs),),
        (feature_rows[:, :half], jnp.where(me == 0, self_rows, cross_rows), common),
        (feature_rows[:, half:], jnp.where(me == 0, cross_rows, self_rows), common),
        flipped=True,
    )
    tail_sum = ctx_total(tail).astype(jnp.float32)
    width = w_qkv.shape[2]
    o_qkv = tail_sum[: 3 * width].reshape(3, width, half).swapaxes(1, 2)
    at = 3 * width
    o_obias, o_gain, o_shift = (tail_sum[at + 3 * i : at + 3 * i + 3] for i in range(3))
    o_abias = tail_sum[at + 9 : at + 11]
    hidden_rows = g_fbias.shape[0] // half
    fbias_total = tail_sum[at + 11 : at + 11 + hidden_rows].reshape(-1)
    square_sums = tail_sum[at + 11 + hidden_rows]
    square_total = square_sums[:4] + square_sums[4:8]
    middle_sum, ffn_sum = middle_sum.astype(jnp.float32), ffn_sum.astype(jnp.float32)
    o_out, o_cq, o_ck, o_cv, o_co = (middle_sum[i * width : (i + 1) * width] for i in range(5))
    o_cq = o_cq.T
    o_ckv = jnp.stack([o_ck.T, o_cv.T])
    hidden_width = g_fbias.shape[0]
    o_fin, o_fout = ffn_sum[:hidden_width].T, ffn_sum[hidden_width : 2 * hidden_width]
    entries = rows * inputs.shape[1] * lax.axis_size("fsdp") * lax.axis_size("ctx")
    rms_values = jnp.sqrt(square_total / entries)
    return (
        swapped(result.astype(jnp.bfloat16))[None],
        swapped(input_grad)[None],
        swapped(source_sum)[None],
        rms_values,
        o_qkv,
        o_out,
        o_cq,
        o_ckv,
        o_co,
        o_fin,
        o_fout,
        o_abias,
        fbias_total,
        o_obias,
        o_gain,
        o_shift,
    )


def solution(mesh):
    in_specs = (
        P("fsdp", "ctx", None),
        P("fsdp", "ctx", None),
        P("fsdp", "ctx"),
        P("fsdp"),
        P("fsdp", "ctx", None),
        P(None, "fsdp", "tp"),
        P("tp", "fsdp"),
        P("fsdp", "tp"),
        P(None, "fsdp", "tp"),
        P("tp", "fsdp"),
        P("fsdp", "tp"),
        P("tp", "fsdp"),
        P("fsdp", "tp"),
        P("tp"),
        P(None, "fsdp"),
        P(None, "fsdp"),
        P(None, "fsdp"),
    )
    out_specs = (
        P("fsdp", "ctx", None),
        P("fsdp", "ctx", None),
        P("fsdp", "ctx", None),
        P(),
        P(None, "fsdp", "tp"),
        P("tp", "fsdp"),
        P("fsdp", "tp"),
        P(None, "fsdp", "tp"),
        P("tp", "fsdp"),
        P("fsdp", "tp"),
        P("tp", "fsdp"),
        P("fsdp", "tp"),
        P("tp"),
        P(None, "fsdp"),
        P(None, "fsdp"),
        P(None, "fsdp"),
    )
    return jax.shard_map(
        per_device, mesh=mesh, in_specs=in_specs, out_specs=out_specs, check_vma=False
    )
```
